32 devices in a mesh: groups: 2 (over x), seq: 16 (over z, y, core).
Axes of the slice: x: 2, y: 2, z: 4, core: 2. Of those that a mesh axis runs over, the one named last changes fastest.
Arguments:
- queries: bfloat16 [8192, 768], P(('groups', 'seq')), parts along dimension 0, may hold values from -10 to 10
- keys: bfloat16 [8192, 768], P(('groups', 'seq')), parts along dimension 0, may hold values from -10 to 10
- values: bfloat16 [8192, 768], P(('groups', 'seq')), parts along dimension 0, may hold values from -6 to 6
- grad_out: bfloat16 [8192, 768], P(('groups', 'seq')), parts along dimension 0, may hold values from -6 to 6
- local_span: int32 [16], replicated, may hold values from 64 to 256, as said below
- head_residue: int32 [16], replicated, may hold values from 0 to 15
- valid_count: int32 [2], P('groups'), parts along dimension 0, may hold values from 1024 to 4096
Outputs:
- query_gradient: bfloat16 [8192, 768], P(('groups', 'seq')), parts along dimension 0
- key_gradient: bfloat16 [8192, 768], P(('groups', 'seq')), parts along dimension 0
- value_gradient: bfloat16 [8192, 768], P(('groups', 'seq')), parts along dimension 0
The draws below stay inside these ranges and needn't reach their ends.
There are 2 independent parts, one for each index of `groups`. The reference program is written for one: setup_inputs(seed, part) draws one part's arguments, and reference() takes and returns one part's arrays. A program takes and returns all parts, laid end to end along the dimension named above; an argument that names none is the same for every part. Nothing has to cross between parts.
Inputs may be any that keep to these rules, and one draw needn't show every extreme that they name: `local_span`: each head's local segment length is 256, 128 or 64; the longest and the shortest both occur. Positions from valid_count on are padding tiles.
All inputs are finite; a program needn't handle non-finite values.
Results may differ from the reference program's by a relative error of at most 0.0072.
Values may be sent and summed in bfloat16 or wider, within the bound.
A program may use at most 128 MiB of HBM per device.

```python
import math
import jax
import jax.numpy as jnp
from jax import lax

HEADS = 16
HEAD_DIM = 48
DILATION_STEP = 16
PARTS_IN_WINDOW = 16
TOKENS_PER_SHARD = 256
WIDTH = 768
SEQ_LEN = 4096


def paired_rows(key):
    base = jax.random.fold_in(key, 11)
    key_query, key_key = jax.random.split(base, 2)
    queries_all = jnp.clip(jax.random.normal(key_query, (SEQ_LEN, WIDTH), jnp.float32), -6.0, 6.0)
    keys_all = jnp.clip(jax.random.normal(key_key, (SEQ_LEN, WIDTH), jnp.float32), -6.0, 6.0)
    return (queries_all, keys_all)


def draw_queries(key, part):
    return paired_rows(key)[0].astype(jnp.bfloat16)


def draw_keys(key, part):
    return paired_rows(key)[1].astype(jnp.bfloat16)


def draw_local_span(key, part):
    key_level, key_order = jax.random.split(jax.random.fold_in(key, 3))
    levels = jax.random.randint(key_level, (HEADS,), 0, 3)
    order = jax.random.permutation(key_order, HEADS)
    levels = levels.at[order[0]].set(0).at[order[1]].set(2)
    spans = jnp.where(levels == 0, TOKENS_PER_SHARD, jnp.where(levels == 1, TOKENS_PER_SHARD // 2, TOKENS_PER_SHARD // 4))
    return spans.astype(jnp.int32)


def with_ends(values, stream_key, smallest, largest):
    shape = values.shape
    index_at = [jax.random.randint(jax.random.fold_in(stream_key, axis), (), 0, shape[axis]) for axis in range(len(shape))]
    values = values.at[tuple(index_at)].set(smallest)
    longest = shape.index(max(shape))
    index_at[longest] = (index_at[longest] + 1) % shape[longest]
    return values.at[tuple(index_at)].set(largest)


def block_levels(rng, extent, cuts, low, top_value):
    level = 1.0
    for axis_at, parts in cuts:
        heights = jax.random.uniform(jax.random.fold_in(jax.random.fold_in(rng, 6), axis_at), (parts,), jnp.float32, low / len(cuts), top_value / len(cuts))
        level = level * jnp.repeat(jnp.exp(heights), extent[axis_at] // parts).reshape((-1,) + (1,) * (len(extent) - 1 - axis_at))
    return level


def gaussian(rng, dims, width, most, shards=(), kind=jnp.bfloat16):
    values = width * jax.random.normal(rng, dims, jnp.float32)
    if shards:
        values = values * block_levels(rng, dims, shards, -0.22, 0.18)
    return jnp.clip(values, -most, most).astype(kind)


def setup_inputs(seed: int = 0, part: int = 0) -> dict:
    streams_of = jax.random.split(jax.random.key(seed), 8)
    own_keys = jax.random.split(jax.random.fold_in(streams_of[7], part), 8)
    queries = draw_queries(jax.random.fold_in(jax.random.fold_in(streams_of[7], part), 71), part)
    keys = draw_keys(jax.random.fold_in(jax.random.fold_in(streams_of[7], part), 71), part)
    values = gaussian(own_keys[2], (SEQ_LEN, WIDTH), 1.0, 6.0, ((0, 16),))
    grad_out = gaussian(own_keys[3], (SEQ_LEN, WIDTH), 1.0, 6.0, ((0, 16),))
    local_span = draw_local_span(jax.random.fold_in(streams_of[7], 71), part)
    head_residue = with_ends(jax.random.randint(streams_of[5], (HEADS,), 0, DILATION_STEP), jax.random.fold_in(streams_of[5], 1), 0, DILATION_STEP - 1).astype(jnp.int32)
    valid_count = jax.random.randint(own_keys[6], (1,), SEQ_LEN // 4, SEQ_LEN + 1).astype(jnp.int32)
    return dict(queries=queries, keys=keys, values=values, grad_out=grad_out, local_span=local_span, head_residue=head_residue, valid_count=valid_count)


SCORE_FLOOR = -1e+30
PRECISE_MODE = lax.Precision.HIGHEST

def select_heads(tokens_heads, indicator_matrix):
    grouped = tokens_heads.reshape(tokens_heads.shape[0] // DILATION_STEP, DILATION_STEP, tokens_heads.shape[1], tokens_heads.shape[2])
    return jnp.einsum('trhe,hr->the', grouped, indicator_matrix, precision=PRECISE_MODE)

def select_statistics(stats, indicator_matrix):
    grouped = stats.reshape(stats.shape[0] // DILATION_STEP, DILATION_STEP, stats.shape[1])
    return jnp.einsum('trh,hr->th', grouped, indicator_matrix, precision=PRECISE_MODE)

def distribute_heads(picked, indicator_matrix):
    full_rows = jnp.einsum('the,hr->trhe', picked, indicator_matrix, precision=PRECISE_MODE)
    return full_rows.reshape(-1, picked.shape[1], picked.shape[2])

def distribute_statistics(picked, indicator_matrix):
    full_rows = jnp.einsum('th,hr->trh', picked, indicator_matrix, precision=PRECISE_MODE)
    return full_rows.reshape(-1, picked.shape[1])

def round_half(values_f):
    return lax.optimization_barrier(values_f.astype(jnp.bfloat16)).astype(jnp.float32)

def reference(queries, keys, values, grad_out, local_span, head_residue, valid_count):
    sequence_rows = queries.shape[0]
    hidden_width = queries.shape[1]
    score_scale = 1.0 / math.sqrt(HEAD_DIM)
    mask_count_total = valid_count[0]
    query_complete = queries.astype(jnp.float32).reshape(sequence_rows, HEADS, HEAD_DIM)
    key_complete = keys.astype(jnp.float32).reshape(sequence_rows, HEADS, HEAD_DIM)
    value_complete = values.astype(jnp.float32).reshape(sequence_rows, HEADS, HEAD_DIM)
    gradient_bundle = grad_out.astype(jnp.float32).reshape(sequence_rows, HEADS, HEAD_DIM)
    indicator_matrix = (head_residue[:, None] == jnp.arange(DILATION_STEP, dtype=jnp.int32)[None, :]).astype(jnp.float32)
    positions = jnp.arange(sequence_rows, dtype=jnp.int32)
    row_mask = positions < mask_count_total
    block_count = sequence_rows // TOKENS_PER_SHARD

    def blocked(array):
        return array.reshape((block_count, TOKENS_PER_SHARD) + array.shape[1:])
    inner = jnp.arange(TOKENS_PER_SHARD, dtype=jnp.int32)
    segment_of = inner[None, :] // local_span[:, None]
    same_local = segment_of[:, :, None] == segment_of[:, None, :]

    def local_scores(query_blk, key_blk):
        return jnp.einsum('ihe,jhe->hij', query_blk, key_blk, precision=PRECISE_MODE) * score_scale

    def local_stats(operands):
        query_blk, key_blk, valid_blk = operands
        scores = local_scores(query_blk, key_blk)
        allowed = same_local & valid_blk[None, None, :]
        running_maximum = lax.optimization_barrier(jnp.max(jnp.where(allowed, scores, SCORE_FLOOR), axis=2))
        row_count_total = lax.optimization_barrier(jnp.sum(jnp.where(allowed, jnp.exp(scores - running_maximum[:, :, None]), 0.0), axis=2))
        return jnp.transpose(running_maximum + jnp.log(row_count_total + 1.0 - valid_blk.astype(jnp.float32)[None, :]))
    dense_logsumexp = lax.map(local_stats, (blocked(query_complete), blocked(key_complete), blocked(row_mask)))
    dense_logsumexp = dense_logsumexp.reshape(sequence_rows, HEADS)
    thinned_probes = select_heads(query_complete, indicator_matrix)
    sparse_keys = select_heads(key_complete, indicator_matrix)
    sparse_values = select_heads(value_complete, indicator_matrix)
    sparse_output_gradient = select_heads(gradient_bundle, indicator_matrix)
    sparse_positions = jnp.arange(sequence_rows // DILATION_STEP, dtype=jnp.int32)[:, None] * DILATION_STEP + head_residue[None, :]
    sparse_row_mask = sparse_positions < mask_count_total
    sparse_segment = sparse_positions // (PARTS_IN_WINDOW * TOKENS_PER_SHARD)
    dense_sparse_logsumexp = select_statistics(dense_logsumexp, indicator_matrix)

    def head_split(array):
        return jnp.swapaxes(array, 0, 1)

    def sparse_branch_forward(operands):
        query_h, key_h, value_h, head_mask, segment_h, dense_head_output = operands
        scores = jnp.dot(query_h, key_h.T, precision=PRECISE_MODE) * score_scale
        allowed = (segment_h[:, None] == segment_h[None, :]) & head_mask[None, :]
        running_maximum = lax.optimization_barrier(jnp.max(jnp.where(allowed, scores, SCORE_FLOOR), axis=1))
        row_count_total = lax.optimization_barrier(jnp.sum(jnp.where(allowed, jnp.exp(scores - running_maximum[:, None]), 0.0), axis=1))
        sparse_logsumexp = running_maximum + jnp.log(row_count_total + 1.0 - head_mask.astype(jnp.float32))
        merged_output = jnp.where(head_mask, jnp.logaddexp(dense_head_output, sparse_logsumexp), 0.0)
        weight = jnp.where(allowed & head_mask[:, None], jnp.exp(scores - merged_output[:, None]), 0.0)
        return (merged_output, jnp.dot(weight, value_h, precision=PRECISE_MODE))
    merged_head_output, sparse_head_output = lax.map(sparse_branch_forward, (head_split(thinned_probes), head_split(sparse_keys), head_split(sparse_values), sparse_row_mask.T, sparse_segment.T, dense_sparse_logsumexp.T))
    merged_output = merged_head_output.T
    global_output = distribute_heads(head_split(sparse_head_output), indicator_matrix)
    complete_logsumexp = jnp.where(row_mask[:, None], dense_logsumexp + distribute_statistics(merged_output - dense_sparse_logsumexp, indicator_matrix), 0.0)

    def local_backward(operands):
        query_blk, key_blk, value_blk, grad_blk, lse_blk, glob_blk, valid_blk = operands
        scores = local_scores(query_blk, key_blk)
        allowed = same_local & valid_blk[None, None, :] & valid_blk[None, :, None]
        weight = jnp.where(allowed, jnp.exp(scores - jnp.transpose(lse_blk)[:, :, None]), 0.0)
        weight_half = round_half(weight)
        output = jnp.einsum('hij,jhe->ihe', weight_half, value_blk, precision=PRECISE_MODE) + glob_blk
        delta_blk = jnp.where(valid_blk[:, None], lax.optimization_barrier(jnp.sum(grad_blk * output, axis=2)), 0.0)
        grad_value = jnp.einsum('hij,ihe->jhe', weight_half, grad_blk, precision=PRECISE_MODE)
        dprod = jnp.einsum('ihe,jhe->hij', grad_blk, value_blk, precision=PRECISE_MODE)
        logit_derivative = round_half(weight * (dprod - jnp.transpose(delta_blk)[:, :, None]))
        grad_query = score_scale * jnp.einsum('hij,jhe->ihe', logit_derivative, key_blk, precision=PRECISE_MODE)
        grad_key = score_scale * jnp.einsum('hij,ihe->jhe', logit_derivative, query_blk, precision=PRECISE_MODE)
        return (grad_query, grad_key, grad_value, delta_blk)
    dense_query_gradient, dense_key_gradient, dense_value_gradient, row_delta = lax.map(local_backward, (blocked(query_complete), blocked(key_complete), blocked(value_complete), blocked(gradient_bundle), blocked(complete_logsumexp), blocked(global_output), blocked(row_mask)))
    shape_full = (sequence_rows, HEADS, HEAD_DIM)
    dense_query_gradient = dense_query_gradient.reshape(shape_full)
    dense_key_gradient = dense_key_gradient.reshape(shape_full)
    dense_value_gradient = dense_value_gradient.reshape(shape_full)
    row_delta = row_delta.reshape(sequence_rows, HEADS)
    sparse_row_delta = select_statistics(row_delta, indicator_matrix)

    def sparse_branch_backward(operands):
        query_h, key_h, value_h, grad_h, head_mask, segment_h, combined_row, delta_row = operands
        scores = jnp.dot(query_h, key_h.T, precision=PRECISE_MODE) * score_scale
        allowed = (segment_h[:, None] == segment_h[None, :]) & head_mask[None, :] & head_mask[:, None]
        weight = jnp.where(allowed, jnp.exp(scores - combined_row[:, None]), 0.0)
        weight_half = round_half(weight)
        grad_value = jnp.dot(weight_half.T, grad_h, precision=PRECISE_MODE)
        dprod = jnp.dot(grad_h, value_h.T, precision=PRECISE_MODE)
        logit_derivative = round_half(weight * (dprod - delta_row[:, None]))
        grad_query = score_scale * jnp.dot(logit_derivative, key_h, precision=PRECISE_MODE)
        grad_key = score_scale * jnp.dot(logit_derivative.T, query_h, precision=PRECISE_MODE)
        return (grad_query, grad_key, grad_value)
    sparse_query_gradient, sparse_key_gradient, sparse_value_gradient = lax.map(sparse_branch_backward, (head_split(thinned_probes), head_split(sparse_keys), head_split(sparse_values), head_split(sparse_output_gradient), sparse_row_mask.T, sparse_segment.T, merged_output.T, sparse_row_delta.T))
    query_gradient = (dense_query_gradient + distribute_heads(head_split(sparse_query_gradient), indicator_matrix)).astype(jnp.bfloat16).reshape(sequence_rows, hidden_width)
    key_gradient = (dense_key_gradient + distribute_heads(head_split(sparse_key_gradient), indicator_matrix)).astype(jnp.bfloat16).reshape(sequence_rows, hidden_width)
    value_gradient = (dense_value_gradient + distribute_heads(head_split(sparse_value_gradient), indicator_matrix)).astype(jnp.bfloat16).reshape(sequence_rows, hidden_width)
    return (query_gradient, key_gradient, value_gradient)
```

```python
import math

import jax
import jax.numpy as jnp
from jax import lax
from jax.experimental import pallas as pl
from jax.experimental.pallas import tpu as pltpu
from jax.sharding import PartitionSpec as P

STEP = 16
WINDOW = 16
FLOOR = -1e30
LOG2E = 1.4426950408889634
EARLY_HEADS = 6

BF = jnp.bfloat16
F32 = jnp.float32


def nn(a, b):
    return lax.dot_general(a, b, (((1,), (0,)), ((), ())), preferred_element_type=F32)


def nt(a, b):
    return lax.dot_general(a, b, (((1,), (1,)), ((), ())), preferred_element_type=F32)


def tn(a, b):
    return lax.dot_general(a, b, (((0,), (0,)), ((), ())), preferred_element_type=F32)


def parts_of(x, count):
    out = []
    for _ in range(count - 1):
        head = x.astype(BF).astype(F32)
        out.append(head)
        x = x - head
    out.append(x)
    return out


def rows_block(rows, height, width):
    at = lax.broadcasted_iota(jnp.int32, (height, width), 0)
    block = jnp.zeros((height, width), F32)
    for n, row in enumerate(rows):
        block = jnp.where(at == n, row, block)
    return block


def kernel(
    span_ref, res_ref, count_ref, q_ref, k_ref, v_ref, g_ref,
    dq_ref, dk_ref, dv_ref,
    qt, kt, vt, gt, dqt, dkt, dvt, qb, gb, pick, far, pb, dpb,
    send1, recv1, send2, recv2, ss1, rs1, ss2, rs2,
):
    tokens, width = q_ref.shape
    heads = span_ref.shape[0]
    dim = width // heads
    few = tokens // STEP
    chosen = heads * few
    scale = 1.0 / math.sqrt(dim)
    scale2 = scale * LOG2E
    me = lax.axis_index("seq")
    base = (me // WINDOW) * WINDOW
    my = me - base
    count = count_ref[0]

    def partner(n):
        return lax.rem(my + n, WINDOW)

    barrier = pltpu.get_barrier_semaphore()

    def greet(n, carry):
        pl.semaphore_signal(
            barrier, inc=1, device_id={"seq": base + partner(n)},
            device_id_type=pl.DeviceIdType.MESH,
        )
        return carry

    lax.fori_loop(1, WINDOW, greet, 0)

    def block_of(n):
        return pl.ds(pl.multiple_of(n * few, few), few)

    def exchange(n, source, target, send_sem, recv_sem):
        to = partner(n)
        return pltpu.make_async_remote_copy(
            src_ref=source.at[block_of(to)],
            dst_ref=target.at[block_of(my)],
            send_sem=send_sem.at[n],
            recv_sem=recv_sem.at[n],
            device_id={"seq": base + to},
            device_id_type=pl.DeviceIdType.MESH,
        )

    def start_all(*args):
        def step(n, carry):
            exchange(n, *args).start()
            return carry

        lax.fori_loop(1, WINDOW, step, 0)

    def wait_all(*args):
        def step(n, carry):
            exchange(n, *args).wait()
            return carry

        lax.fori_loop(1, WINDOW, step, 0)

    lane = lax.broadcasted_iota(jnp.int32, (1, chosen), 1)
    lane_head = lane // few
    lane_res = jnp.zeros((1, chosen), jnp.int32)
    lane_span = jnp.zeros((1, chosen), jnp.int32)
    for h in range(heads):
        lane_res = jnp.where(lane_head == h, res_ref[h], lane_res)
        lane_span = jnp.where(lane_head == h, span_ref[h], lane_span)
    lane_token = (lane % few) * STEP + lane_res
    row = lax.broadcasted_iota(jnp.int32, (tokens, tokens), 0)
    col = lax.broadcasted_iota(jnp.int32, (tokens, tokens), 1)
    start = me * tokens
    huge = jnp.int32(1 << 20)
    row_ok = row + start < count
    far[...] = jnp.where(row_ok, row ^ col, huge)
    pick[...] = (row == lane_token).astype(F32).astype(BF)

    qt[...] = q_ref[...].T
    kt[...] = k_ref[...].T
    vt[...] = v_ref[...].T
    gt[...] = g_ref[...].T

    def picked(source, keep):
        full = nn(source[...], pick[...])
        total = jnp.zeros((dim, chosen), F32)
        for h in range(heads):
            part = jnp.where(lane_head == h, full[h * dim : (h + 1) * dim], 0.0)
            if keep is not None:
                keep[h * dim : (h + 1) * dim, :] = part.astype(BF)
            total = total + part
        return total

    q_few = picked(qt, qb)
    g_few = picked(gt, gb)
    k_few = picked(kt, None)
    v_few = picked(vt, None)

    mask = jnp.where(row_ok, row ^ lane_token, huge) < lane_span
    s = jnp.where(mask, nn(k_ref[...], qb[...]) * scale2, FLOOR)
    top = jnp.max(s, axis=0, keepdims=True)
    p = jnp.exp2(s - top)
    total = jnp.sum(p, axis=0, keepdims=True)
    p = p * (1.0 / total)
    dp = nn(v_ref[...], gb[...])
    local_lse = top + jnp.log(total) * LOG2E
    local_delta = jnp.sum(p * dp, axis=0, keepdims=True)
    pb[...] = p
    dpb[...] = dp
    tail = chosen - 4 * dim
    stats = rows_block(parts_of(local_lse, 3) + parts_of(local_delta, 2), tail, chosen)
    packed = jnp.concatenate([q_few, k_few, v_few, g_few, stats], axis=0)
    send1[...] = packed.T.astype(BF)

    pl.semaphore_wait(barrier, WINDOW - 1)
    start_all(send1, recv1, ss1, rs1)
    recv1[block_of(my), :] = send1[block_of(my), :]

    query_ok = lane + start < count

    def local_head(h, carry):
        at = pl.ds(pl.multiple_of(h * dim, 16), dim)
        qh, kh, vh, gh = qt[at, :], kt[at, :], vt[at, :], gt[at, :]
        s = jnp.where(far[...] < span_ref[h], tn(kh, qh) * scale2, FLOOR)
        top = jnp.max(s, axis=0, keepdims=True)
        p = jnp.exp2(s - top)
        inverse = 1.0 / jnp.sum(p, axis=0, keepdims=True)
        dp = tn(vh, gh)
        delta = jnp.sum(p * dp, axis=0, keepdims=True) * inverse
        keep = query_ok & (lane % STEP != res_ref[h])
        w = p * jnp.where(keep, inverse, 0.0)
        ds = (w * (dp - delta)).astype(BF)
        dqt[at, :] = nn(kh, ds) * scale
        dkt[at, :] = nt(qh, ds) * scale
        dvt[at, :] = nt(gh, w.astype(BF))
        return carry

    lax.fori_loop(0, EARLY_HEADS, local_head, 0)

    wait_all(send1, recv1, ss1, rs1)
    got = recv1[...].astype(F32).T
    got_half = got.astype(BF)
    qh, kh = got_half[0:dim], got_half[dim : 2 * dim]
    vh, gh = got_half[2 * dim : 3 * dim], got_half[3 * dim : 4 * dim]
    at = 4 * dim
    local_lse = got[at : at + 1] + got[at + 1 : at + 2] + got[at + 2 : at + 3]
    local_delta = got[at + 3 : at + 4] + got[at + 4 : at + 5]
    limit = count - base * tokens - res_ref[my]
    s = jnp.where(row * STEP < limit, tn(kh, qh) * scale2, FLOOR)
    top = jnp.max(s, axis=0, keepdims=True)
    p = jnp.exp2(s - top)
    total = jnp.sum(p, axis=0, keepdims=True)
    dilated_lse = top + jnp.log(total) * LOG2E
    most = jnp.maximum(local_lse, dilated_lse)
    both = most + jnp.log(jnp.exp2(local_lse - most) + jnp.exp2(dilated_lse - most)) * LOG2E
    here_ok = lane * STEP < limit
    local_part = jnp.where(here_ok, jnp.exp2(local_lse - both), 0.0)
    u = p * jnp.where(here_ok, jnp.exp2(top - both), 0.0)
    dp = tn(vh, gh)
    delta = local_part * local_delta + jnp.sum(u * dp, axis=0, keepdims=True)
    delta = jnp.where(here_ok, delta, 0.0)
    ds = (u * (dp - delta)).astype(BF)
    stats = rows_block(parts_of(local_part, 2) + parts_of(delta, 2), chosen - 3 * dim, chosen)
    packed = jnp.concatenate(
        [nn(kh, ds) * scale, nt(qh, ds) * scale, nt(gh, u.astype(BF)), stats], axis=0
    )
    send2[...] = packed.T.astype(BF)
    start_all(send2, recv2, ss2, rs2)
    recv2[block_of(my), :] = send2[block_of(my), :]

    lax.fori_loop(EARLY_HEADS, heads, local_head, 0)

    wait_all(send2, recv2, ss2, rs2)
    back = recv2[...].astype(F32).T
    at = 3 * dim
    local_part = back[at : at + 1] + back[at + 1 : at + 2]
    delta = back[at + 2 : at + 3] + back[at + 3 : at + 4]
    w = pb[...] * local_part
    ds = (w * (dpb[...] - delta)).astype(BF)
    wide = nn(kt[...], ds) * scale
    dq_few, dk_few, dv_few = back[0:dim], back[dim : 2 * dim], back[2 * dim : 3 * dim]

    def spread(piece_of):
        pieces = [
            jnp.where(lane_head == h, piece_of(h), 0.0).astype(BF) for h in range(heads)
        ]
        return nt(jnp.concatenate(pieces, axis=0), pick[...])

    dq = dqt[...] + spread(lambda h: wide[h * dim : (h + 1) * dim] + dq_few)
    dq_ref[...] = dq.T.astype(BF)
    dk = dkt[...] + nt(qb[...], ds) * scale + spread(lambda h: dk_few)
    dk_ref[...] = dk.T.astype(BF)
    dv = dvt[...] + nt(gb[...], w.astype(BF)) + spread(lambda h: dv_few)
    dv_ref[...] = dv.T.astype(BF)


def shards(queries, keys, values, grad_out, local_span, head_residue, valid_count):
    tokens, width = queries.shape
    heads = local_span.shape[0]
    chosen = heads * (tokens // STEP)
    assert heads == WINDOW and chosen == tokens
    smem = pl.BlockSpec(memory_space=pltpu.SMEM)
    vmem = pl.BlockSpec(memory_space=pltpu.VMEM)
    out = jax.ShapeDtypeStruct((tokens, width), BF)
    return pl.pallas_call(
        kernel,
        out_shape=(out, out, out),
        in_specs=[smem] * 3 + [vmem] * 4,
        out_specs=(vmem, vmem, vmem),
        scratch_shapes=[pltpu.VMEM((width, tokens), BF)] * 4
        + [pltpu.VMEM((width, tokens), F32)] * 3
        + [pltpu.VMEM((width, chosen), BF)] * 2
        + [
            pltpu.VMEM((tokens, chosen), BF),
            pltpu.VMEM((tokens, tokens), jnp.int32),
            pltpu.VMEM((tokens, chosen), F32),
            pltpu.VMEM((tokens, chosen), F32),
        ]
        + [pltpu.VMEM((chosen, chosen), BF)] * 4
        + [pltpu.SemaphoreType.DMA((WINDOW,))] * 4,
        compiler_params=pltpu.CompilerParams(
            collective_id=0, has_side_effects=True, vmem_limit_bytes=40 * 2**20
        ),
    )(local_span, head_residue, valid_count, queries, keys, values, grad_out)


def solution(mesh):
    rows = P(("groups", "seq"), None)
    return jax.shard_map(
        shards,
        mesh=mesh,
        in_specs=(rows, rows, rows, rows, P(), P(), P("groups")),
        out_specs=(rows, rows, rows),
        check_vma=False,
    )
```

```python
import math

import jax
import jax.numpy as jnp
from jax import lax
from jax.experimental import pallas as pl
from jax.experimental.pallas import tpu as pltpu
from jax.sharding import PartitionSpec as P

STEP = 16
WINDOW = 16
FLOOR = -1e30
LOG2E = 1.4426950408889634
EARLY_HEADS = 6
VMEM_LIMIT = 63 * 2**20

BF = jnp.bfloat16
F32 = jnp.float32


def nn(a, b):
    return lax.dot_general(a, b, (((1,), (0,)), ((), ())), preferred_element_type=F32)


def nt(a, b):
    return lax.dot_general(a, b, (((1,), (1,)), ((), ())), preferred_element_type=F32)


def tn(a, b):
    return lax.dot_general(a, b, (((0,), (0,)), ((), ())), preferred_element_type=F32)


def parts_of(x, count):
    out = []
    for _ in range(count - 1):
        head = x.astype(BF).astype(F32)
        out.append(head)
        x = x - head
    out.append(x)
    return out


def rows_block(rows, height, width):
    at = lax.broadcasted_iota(jnp.int32, (height, width), 0)
    block = jnp.zeros((height, width), F32)
    for n, row in enumerate(rows):
        block = jnp.where(at == n, row, block)
    return block


def kernel(
    span_ref, res_ref, count_ref, q_hbm, k_hbm, v_hbm, g_hbm,
    dq_hbm, dk_hbm, dv_hbm,
    dq_ref, dk_ref, dv_ref, store_sem, q_ref, k_ref, v_ref, g_ref, load_sem, qt, kt, vt, gt, dqt, dkt, dvt, qb, gb, pick, far, pb, dpb,
    send1, recv1, send2, recv2, ss1, rs1, ss2, rs2,
):
    tokens, width = q_ref.shape
    heads = span_ref.shape[0]
    dim = width // heads
    few = tokens // STEP
    chosen = heads * few
    scale = 1.0 / math.sqrt(dim)
    scale2 = scale * LOG2E
    me = lax.axis_index("seq")
    base = (me // WINDOW) * WINDOW
    my = me - base
    count = count_ref[0]
    loads = [
        pltpu.make_async_copy(source, target, load_sem.at[n])
        for n, (source, target) in enumerate(
            ((q_hbm, q_ref), (g_hbm, g_ref), (k_hbm, k_ref), (v_hbm, v_ref))
        )
    ]
    for load in loads:
        load.start()

    def partner(n):
        return lax.rem(my + n, WINDOW)

    barrier = pltpu.get_barrier_semaphore()

    def greet(n, carry):
        pl.semaphore_signal(
            barrier, inc=1, device_id={"seq": base + partner(n)},
            device_id_type=pl.DeviceIdType.MESH,
        )
        return carry

    lax.fori_loop(1, WINDOW, greet, 0)

    def block_of(n):
        return pl.ds(pl.multiple_of(n * few, few), few)

    def exchange(n, source, target, send_sem, recv_sem):
        to = partner(n)
        return pltpu.make_async_remote_copy(
            src_ref=source.at[block_of(to)],
            dst_ref=target.at[block_of(my)],
            send_sem=send_sem.at[n],
            recv_sem=recv_sem.at[n],
            device_id={"seq": base + to},
            device_id_type=pl.DeviceIdType.MESH,
        )

    def start_all(*args):
        def step(n, carry):
            exchange(n, *args).start()
            return carry

        lax.fori_loop(1, WINDOW, step, 0)

    def wait_all(*args):
        def step(n, carry):
            exchange(n, *args).wait()
            return carry

        lax.fori_loop(1, WINDOW, step, 0)

    lane = lax.broadcasted_iota(jnp.int32, (1, chosen), 1)
    lane_head = lane // few
    lane_res = jnp.zeros((1, chosen), jnp.int32)
    lane_span = jnp.zeros((1, chosen), jnp.int32)
    for h in range(heads):
        lane_res = jnp.where(lane_head == h, res_ref[h], lane_res)
        lane_span = jnp.where(lane_head == h, span_ref[h], lane_span)
    lane_token = (lane % few) * STEP + lane_res
    row = lax.broadcasted_iota(jnp.int32, (tokens, tokens), 0)
    col = lax.broadcasted_iota(jnp.int32, (tokens, tokens), 1)
    start = me * tokens
    huge = jnp.int32(1 << 20)
    row_ok = row + start < count
    far[...] = jnp.where(row_ok, row ^ col, huge)
    pick[...] = (row == lane_token).astype(F32).astype(BF)

    for load, source, target in zip(
        loads, (q_ref, g_ref, k_ref, v_ref), (qt, gt, kt, vt)
    ):
        load.wait()
        target[...] = source[...].T

    def picked(source, keep):
        full = nn(source[...], pick[...])
        total = jnp.zeros((dim, chosen), F32)
        for h in range(heads):
            part = jnp.where(lane_head == h, full[h * dim : (h + 1) * dim], 0.0)
            if keep is not None:
                keep[h * dim : (h + 1) * dim, :] = part.astype(BF)
            total = total + part
        return total

    q_few = picked(qt, qb)
    g_few = picked(gt, gb)
    k_few = picked(kt, None)
    v_few = picked(vt, None)

    mask = jnp.where(row_ok, row ^ lane_token, huge) < lane_span
    s = jnp.where(mask, nn(k_ref[...], qb[...]) * scale2, FLOOR)
    top = jnp.max(s, axis=0, keepdims=True)
    p = jnp.exp2(s - top)
    total = jnp.sum(p, axis=0, keepdims=True)
    p = p * (1.0 / total)
    dp = nn(v_ref[...], gb[...])
    local_lse = top + jnp.log(total) * LOG2E
    local_delta = jnp.sum(p * dp, axis=0, keepdims=True)
    pb[...] = p
    dpb[...] = dp
    tail = chosen - 4 * dim
    stats = rows_block(parts_of(local_lse, 3) + parts_of(local_delta, 2), tail, chosen)
    packed = jnp.concatenate([q_few, k_few, v_few, g_few, stats], axis=0)
    send1[...] = packed.T.astype(BF)

    pl.semaphore_wait(barrier, WINDOW - 1)
    start_all(send1, recv1, ss1, rs1)
    recv1[block_of(my), :] = send1[block_of(my), :]

    query_ok = lane + start < count

    def local_head(h, carry):
        at = pl.ds(pl.multiple_of(h * dim, 16), dim)
        qh, kh, vh, gh = qt[at, :], kt[at, :], vt[at, :], gt[at, :]
        s = jnp.where(far[...] < span_ref[h], tn(kh, qh) * scale2, FLOOR)
        top = jnp.max(s, axis=0, keepdims=True)
        p = jnp.exp2(s - top)
        inverse = 1.0 / jnp.sum(p, axis=0, keepdims=True)
        dp = tn(vh, gh)
        delta = jnp.sum(p * dp, axis=0, keepdims=True) * inverse
        keep = query_ok & (lane % STEP != res_ref[h])
        w = p * jnp.where(keep, inverse, 0.0)
        ds = (w * (dp - delta)).astype(BF)
        dqt[at, :] = nn(kh, ds) * scale
        dkt[at, :] = nt(qh, ds) * scale
        dvt[at, :] = nt(gh, w.astype(BF))
        return carry

    lax.fori_loop(0, EARLY_HEADS, local_head, 0, unroll=2)

    wait_all(send1, recv1, ss1, rs1)
    got = recv1[...].astype(F32).T
    got_half = got.astype(BF)
    qh, kh = got_half[0:dim], got_half[dim : 2 * dim]
    vh, gh = got_half[2 * dim : 3 * dim], got_half[3 * dim : 4 * dim]
    at = 4 * dim
    local_lse = got[at : at + 1] + got[at + 1 : at + 2] + got[at + 2 : at + 3]
    local_delta = got[at + 3 : at + 4] + got[at + 4 : at + 5]
    limit = count - base * tokens - res_ref[my]
    s = jnp.where(row * STEP < limit, tn(kh, qh) * scale2, FLOOR)
    top = jnp.max(s, axis=0, keepdims=True)
    p = jnp.exp2(s - top)
    total = jnp.sum(p, axis=0, keepdims=True)
    dilated_lse = top + jnp.log(total) * LOG2E
    most = jnp.maximum(local_lse, dilated_lse)
    both = most + jnp.log(jnp.exp2(local_lse - most) + jnp.exp2(dilated_lse - most)) * LOG2E
    here_ok = lane * STEP < limit
    local_part = jnp.where(here_ok, jnp.exp2(local_lse - both), 0.0)
    u = p * jnp.where(here_ok, jnp.exp2(top - both), 0.0)
    dp = tn(vh, gh)
    delta = local_part * local_delta + jnp.sum(u * dp, axis=0, keepdims=True)
    delta = jnp.where(here_ok, delta, 0.0)
    ds = (u * (dp - delta)).astype(BF)
    stats = rows_block(parts_of(local_part, 2) + parts_of(delta, 2), chosen - 3 * dim, chosen)
    packed = jnp.concatenate(
        [nn(kh, ds) * scale, nt(qh, ds) * scale, nt(gh, u.astype(BF)), stats], axis=0
    )
    send2[...] = packed.T.astype(BF)
    start_all(send2, recv2, ss2, rs2)
    recv2[block_of(my), :] = send2[block_of(my), :]

    lax.fori_loop(EARLY_HEADS, heads, local_head, 0, unroll=2)

    wait_all(send2, recv2, ss2, rs2)
    back = recv2[...].astype(F32).T
    at = 3 * dim
    local_part = back[at : at + 1] + back[at + 1 : at + 2]
    delta = back[at + 2 : at + 3] + back[at + 3 : at + 4]
    w = pb[...] * local_part
    ds = (w * (dpb[...] - delta)).astype(BF)
    wide = nn(kt[...], ds) * scale
    dq_few, dk_few, dv_few = back[0:dim], back[dim : 2 * dim], back[2 * dim : 3 * dim]

    def spread(piece_of):
        pieces = [
            jnp.where(lane_head == h, piece_of(h), 0.0).astype(BF) for h in range(heads)
        ]
        return nt(jnp.concatenate(pieces, axis=0), pick[...])

    def store(n, source, target):
        copy = pltpu.make_async_copy(source, target, store_sem.at[n])
        copy.start()
        return copy

    dq = dqt[...] + spread(lambda h: wide[h * dim : (h + 1) * dim] + dq_few)
    dq_ref[...] = dq.astype(BF)
    store_dq = store(0, dq_ref, dq_hbm)
    dk = dkt[...] + nt(qb[...], ds) * scale + spread(lambda h: dk_few)
    dk_ref[...] = dk.astype(BF)
    store_dk = store(1, dk_ref, dk_hbm)
    dv = dvt[...] + nt(gb[...], w.astype(BF)) + spread(lambda h: dv_few)
    dv_ref[...] = dv.astype(BF)
    store_dv = store(2, dv_ref, dv_hbm)
    store_dq.wait()
    store_dk.wait()
    store_dv.wait()


def finish(a_in, b_in, c_in, a_out, b_out, c_out, sources, targets, load_sem, store_sem):
    loads = [
        pltpu.make_async_copy(ref, sources.at[n], load_sem.at[n])
        for n, ref in enumerate((a_in, b_in, c_in))
    ]
    for load in loads:
        load.start()
    stores = [
        pltpu.make_async_copy(targets.at[n], ref, store_sem.at[n])
        for n, ref in enumerate((a_out, b_out, c_out))
    ]
    for n in range(3):
        loads[n].wait()
        targets[n] = sources[n].T
        stores[n].start()
    for store in stores:
        store.wait()


def shards(queries, keys, values, grad_out, local_span, head_residue, valid_count):
    tokens, width = queries.shape
    heads = local_span.shape[0]
    chosen = heads * (tokens // STEP)
    assert heads == WINDOW and chosen == tokens
    smem = pl.BlockSpec(memory_space=pltpu.SMEM)
    vmem = pl.BlockSpec(memory_space=pltpu.VMEM)
    hbm = pl.BlockSpec(memory_space=pltpu.MemorySpace.HBM)
    out = jax.ShapeDtypeStruct((tokens, width), BF)
    turned = jax.ShapeDtypeStruct((width, tokens), BF)
    gradients = pl.pallas_call(
        kernel,
        out_shape=(turned, turned, turned),
        in_specs=[smem] * 3 + [hbm] * 4,
        out_specs=(hbm, hbm, hbm),
        scratch_shapes=[pltpu.VMEM((width, tokens), BF)] * 3
        + [pltpu.SemaphoreType.DMA((3,))]
        + [pltpu.VMEM((tokens, width), BF)] * 4
        + [pltpu.SemaphoreType.DMA((4,))]
        + [pltpu.VMEM((width, tokens), BF)] * 4
        + [pltpu.VMEM((width, tokens), F32)] * 3
        + [pltpu.VMEM((width, chosen), BF)] * 2
        + [
            pltpu.VMEM((tokens, chosen), BF),
            pltpu.VMEM((tokens, tokens), jnp.int32),
            pltpu.VMEM((tokens, chosen), F32),
            pltpu.VMEM((tokens, chosen), F32),
        ]
        + [pltpu.VMEM((chosen, chosen), BF)] * 4
        + [pltpu.SemaphoreType.DMA((WINDOW,))] * 4,
        compiler_params=pltpu.CompilerParams(
            collective_id=0, has_side_effects=True, vmem_limit_bytes=VMEM_LIMIT
        ),
    )(local_span, head_residue, valid_count, queries, keys, values, grad_out)
    return pl.pallas_call(
        finish,
        out_shape=(out, out, out),
        in_specs=[hbm] * 3,
        out_specs=(hbm, hbm, hbm),
        scratch_shapes=[
            pltpu.VMEM((3, width, tokens), BF),
            pltpu.VMEM((3, tokens, width), BF),
            pltpu.SemaphoreType.DMA((3,)),
            pltpu.SemaphoreType.DMA((3,)),
        ],
        compiler_params=pltpu.CompilerParams(vmem_limit_bytes=VMEM_LIMIT),
    )(*gradients)


def solution(mesh):
    rows = P(("groups", "seq"), None)
    return jax.shard_map(
        shards,
        mesh=mesh,
        in_specs=(rows, rows, rows, rows, P(), P(), P("groups")),
        out_specs=(rows, rows, rows),
        check_vma=False,
    )
```

```python
import math

import jax
import jax.numpy as jnp
from jax import lax
from jax.experimental import pallas as pl
from jax.experimental.pallas import tpu as pltpu
from jax.sharding import PartitionSpec as P

STEP = 16
WINDOW = 16
FLOOR = -1e30
LOG2E = 1.4426950408889634
EARLY_HEADS = 6
VMEM_LIMIT = 63 * 2**20

BF = jnp.bfloat16
F32 = jnp.float32


def nn(a, b):
    return lax.dot_general(a, b, (((1,), (0,)), ((), ())), preferred_element_type=F32)


def nt(a, b):
    return lax.dot_general(a, b, (((1,), (1,)), ((), ())), preferred_element_type=F32)


def tn(a, b):
    return lax.dot_general(a, b, (((0,), (0,)), ((), ())), preferred_element_type=F32)


def parts_of(x, count):
    out = []
    for _ in range(count - 1):
        head = x.astype(BF).astype(F32)
        out.append(head)
        x = x - head
    out.append(x)
    return out


def rows_block(rows, height, width):
    at = lax.broadcasted_iota(jnp.int32, (height, width), 0)
    block = jnp.zeros((height, width), F32)
    for n, row in enumerate(rows):
        block = jnp.where(at == n, row, block)
    return block


def one_hot(condition):
    return condition.astype(F32).astype(BF)


def fold_matrix(heads, dim, wide, offset):
    feature = lax.broadcasted_iota(jnp.int32, (dim, wide), 1)
    column = lax.broadcasted_iota(jnp.int32, (dim, wide), 0)
    return jnp.concatenate([one_hot(feature == column + offset)] * heads, axis=0)


def stat_matrix(wide, offset):
    feature = lax.broadcasted_iota(jnp.int32, (16, wide), 1)
    return one_hot(feature == lax.broadcasted_iota(jnp.int32, (16, wide), 0) + offset)


def lane_tokens(res_ref, chosen, few):
    lane = lax.broadcasted_iota(jnp.int32, (1, chosen), 1)
    residue = jnp.zeros((1, chosen), jnp.int32)
    for h in range(chosen // few):
        residue = jnp.where(lane // few == h, res_ref[h], residue)
    return (lane % few) * STEP + residue


def own_columns(chosen, width, few, dim):
    row = lax.broadcasted_iota(jnp.int32, (chosen, 1), 0)
    column = lax.broadcasted_iota(jnp.int32, (1, width), 1)
    return (row // few) == (column // dim)


def kernel(
    span_ref, res_ref, count_ref, q_hbm, k_hbm, v_hbm, g_hbm,
    recv2, pb_hbm, dpb_hbm, qb_hbm, gb_hbm, dq_hbm, dk_hbm, dv_hbm,
    q_ref, k_ref, v_ref, g_ref, load_sem, store_sem, own_sem,
    qt, kt, vt, gt, dqt, dkt, dvt, dq_ref, dk_ref, dv_ref, qb, gb, far, pb, dpb,
    send1, recv1, send2, ss1, rs1, ss2, rs2,
):
    tokens, width = q_ref.shape
    heads = span_ref.shape[0]
    dim = width // heads
    few = tokens // STEP
    chosen = heads * few
    scale = 1.0 / math.sqrt(dim)
    scale2 = scale * LOG2E
    me = lax.axis_index("seq")
    base = (me // WINDOW) * WINDOW
    my = me - base
    count = count_ref[0]
    loads = [
        pltpu.make_async_copy(source, target, load_sem.at[n])
        for n, (source, target) in enumerate(
            ((q_hbm, q_ref), (g_hbm, g_ref), (k_hbm, k_ref), (v_hbm, v_ref))
        )
    ]
    for load in loads:
        load.start()

    def partner(n):
        return lax.rem(my + n, WINDOW)

    barrier = pltpu.get_barrier_semaphore()

    def greet(n, carry):
        pl.semaphore_signal(
            barrier, inc=1, device_id={"seq": base + partner(n)},
            device_id_type=pl.DeviceIdType.MESH,
        )
        return carry

    lax.fori_loop(1, WINDOW, greet, 0)

    def block_of(n):
        return pl.ds(pl.multiple_of(n * few, few), few)

    def exchange(n, source, target, send_sem, recv_sem):
        to = partner(n)
        return pltpu.make_async_remote_copy(
            src_ref=source.at[block_of(to)],
            dst_ref=target.at[block_of(my)],
            send_sem=send_sem.at[n],
            recv_sem=recv_sem.at[n],
            device_id={"seq": base + to},
            device_id_type=pl.DeviceIdType.MESH,
        )

    def start_all(*args):
        def step(n, carry):
            exchange(n, *args).start()
            return carry

        lax.fori_loop(1, WINDOW, step, 0)

    def wait_all(*args):
        def step(n, carry):
            exchange(n, *args).wait()
            return carry

        lax.fori_loop(1, WINDOW, step, 0)

    stores = []

    def store(source, target):
        copy = pltpu.make_async_copy(source, target, store_sem.at[len(stores)])
        copy.start()
        stores.append(copy)

    lane = lax.broadcasted_iota(jnp.int32, (1, chosen), 1)
    lane_token = lane_tokens(res_ref, chosen, few)
    lane_span = jnp.zeros((1, chosen), jnp.int32)
    for h in range(heads):
        lane_span = jnp.where(lane // few == h, span_ref[h], lane_span)
    row = lax.broadcasted_iota(jnp.int32, (tokens, tokens), 0)
    col = lax.broadcasted_iota(jnp.int32, (tokens, tokens), 1)
    start = me * tokens
    huge = jnp.int32(1 << 20)
    row_ok = row + start < count
    far[...] = jnp.where(row_ok, row ^ col, huge)
    thin = lax.broadcasted_iota(jnp.int32, (chosen, 1), 0)
    thin_res = jnp.zeros((chosen, 1), jnp.int32)
    for h in range(heads):
        thin_res = jnp.where(thin // few == h, res_ref[h], thin_res)
    pick = one_hot(col == (thin % few) * STEP + thin_res)
    own = own_columns(chosen, width, few, dim)

    def picked(n, order, source, keep):
        loads[order].wait()
        part = jnp.where(own, nn(pick, source[...]), 0.0).astype(BF)
        if keep is not None:
            keep[...] = part
        return nn(part, fold_matrix(heads, dim, chosen, n * dim))

    packed = picked(0, 0, q_ref, qb) + picked(3, 1, g_ref, gb)
    packed = packed + picked(1, 2, k_ref, None)
    mask = jnp.where(row_ok, row ^ lane_token, huge) < lane_span
    s = jnp.where(mask, nt(k_ref[...], qb[...]) * scale2, FLOOR)
    top = jnp.max(s, axis=0, keepdims=True)
    p = jnp.exp2(s - top)
    total = jnp.sum(p, axis=0, keepdims=True)
    p = p * (1.0 / total)
    packed = packed + picked(2, 3, v_ref, None)
    dp = nt(v_ref[...], gb[...])
    local_lse = top + jnp.log(total) * LOG2E
    local_delta = jnp.sum(p * dp, axis=0, keepdims=True)
    pb[...] = p
    dpb[...] = dp
    stat_out = stat_matrix(chosen, 4 * dim)
    stats = rows_block(parts_of(local_lse, 3) + parts_of(local_delta, 2), 16, chosen)
    send1[...] = (packed + tn(stats.astype(BF), stat_out)).astype(BF)

    pl.semaphore_wait(barrier, WINDOW - 1)
    start_all(send1, recv1, ss1, rs1)
    recv1[block_of(my), :] = send1[block_of(my), :]
    store(pb, pb_hbm)
    store(dpb, dpb_hbm)
    store(qb, qb_hbm)
    store(gb, gb_hbm)
    for source, target in zip((q_ref, g_ref, k_ref, v_ref), (qt, gt, kt, vt)):
        target[...] = source[...].T

    query_ok = lane + start < count

    def local_head(h, carry):
        at = pl.ds(pl.multiple_of(h * dim, 16), dim)
        qh, kh, vh, gh = qt[at, :], kt[at, :], vt[at, :], gt[at, :]
        s = jnp.where(far[...] < span_ref[h], tn(kh, qh) * scale2, FLOOR)
        top = jnp.max(s, axis=0, keepdims=True)
        p = jnp.exp2(s - top)
        inverse = 1.0 / jnp.sum(p, axis=0, keepdims=True)
        dp = tn(vh, gh)
        delta = jnp.sum(p * dp, axis=0, keepdims=True) * inverse
        keep = query_ok & (lane % STEP != res_ref[h])
        w = p * jnp.where(keep, inverse, 0.0)
        ds = (w * (dp - delta)).astype(BF)
        dqt[at, :] = nn(kh, ds) * scale
        dkt[at, :] = nt(qh, ds) * scale
        dvt[at, :] = nt(gh, w.astype(BF))
        return carry

    lax.fori_loop(0, EARLY_HEADS, local_head, 0, unroll=2)

    wait_all(send1, recv1, ss1, rs1)
    feature_in = lax.broadcasted_iota(jnp.int32, (chosen, chosen), 0)
    feature_out = lax.broadcasted_iota(jnp.int32, (chosen, chosen), 1)

    def moved(source, target):
        shift = feature_in - feature_out == (source - target) * dim
        inside = (feature_out >= target * dim) & (feature_out < (target + 1) * dim)
        return nn(got, one_hot(shift & inside)).astype(BF)

    got = recv1[...]
    kp, qp, gp = moved(1, 0), moved(0, 1), moved(3, 2)
    stats = nt(stat_out, got)
    local_lse = stats[0:1] + stats[1:2] + stats[2:3]
    local_delta = stats[3:4] + stats[4:5]
    limit = count - base * tokens - res_ref[my]
    s = jnp.where(row * STEP < limit, nt(got, qp) * scale2, FLOOR)
    top = jnp.max(s, axis=0, keepdims=True)
    p = jnp.exp2(s - top)
    total = jnp.sum(p, axis=0, keepdims=True)
    dilated_lse = top + jnp.log(total) * LOG2E
    most = jnp.maximum(local_lse, dilated_lse)
    both = most + jnp.log(jnp.exp2(local_lse - most) + jnp.exp2(dilated_lse - most)) * LOG2E
    here_ok = lane * STEP < limit
    local_part = jnp.where(here_ok, jnp.exp2(local_lse - both), 0.0)
    u = p * jnp.where(here_ok, jnp.exp2(top - both), 0.0)
    dp = nt(got, gp)
    delta = local_part * local_delta + jnp.sum(u * dp, axis=0, keepdims=True)
    delta = jnp.where(here_ok, delta, 0.0)
    ds = (u * (dp - delta)).astype(BF)
    stats = rows_block(parts_of(local_part, 2) + parts_of(delta, 2), 16, chosen)
    packed = (tn(ds, kp) + nn(ds, qp)) * scale + nn(u.astype(BF), gp)
    send2[...] = (packed + tn(stats.astype(BF), stat_matrix(chosen, 3 * dim))).astype(BF)
    start_all(send2, recv2, ss2, rs2)
    own_copy = pltpu.make_async_copy(
        send2.at[block_of(my)], recv2.at[block_of(my)], own_sem.at[0]
    )
    own_copy.start()

    lax.fori_loop(EARLY_HEADS, heads, local_head, 0, unroll=2)

    for source, target, output in (
        (dqt, dq_ref, dq_hbm), (dkt, dk_ref, dk_hbm), (dvt, dv_ref, dv_hbm)
    ):
        target[...] = source[...].astype(BF).T
        store(target, output)
    wait_all(send2, recv2, ss2, rs2)
    own_copy.wait()
    for copy in stores:
        copy.wait()


def finish(
    res_ref, back_hbm, pb_hbm, dpb_hbm, k_hbm, dql_hbm, qb_hbm, dkl_hbm, gb_hbm, dvl_hbm,
    dq_hbm, dk_hbm, dv_hbm,
    back, pb, dpb, k_ref, dql, qb, dkl, gb, dvl, dq_ref, dk_ref, dv_ref, load_sem, store_sem,
):
    tokens, width = k_ref.shape
    heads = res_ref.shape[0]
    dim = width // heads
    few = tokens // STEP
    chosen = heads * few
    scale = 1.0 / math.sqrt(dim)
    sources = (back_hbm, pb_hbm, dpb_hbm, k_hbm, dql_hbm, qb_hbm, dkl_hbm, gb_hbm, dvl_hbm)
    targets = (back, pb, dpb, k_ref, dql, qb, dkl, gb, dvl)
    loads = [
        pltpu.make_async_copy(source, target, load_sem.at[n])
        for n, (source, target) in enumerate(zip(sources, targets))
    ]
    for load in loads:
        load.start()
    row = lax.broadcasted_iota(jnp.int32, (tokens, chosen), 0)
    pick = one_hot(row == lane_tokens(res_ref, chosen, few))
    own = own_columns(chosen, width, few, dim)
    stat_in = stat_matrix(chosen, 3 * dim)
    for load in loads[:3]:
        load.wait()
    got = back[...]
    stats = nt(stat_in, got)
    local_part = stats[0:1] + stats[1:2]
    delta = stats[2:3] + stats[3:4]
    w = pb[...] * local_part
    ds = (w * (dpb[...] - delta)).astype(BF)
    w = w.astype(BF)

    def returned(n):
        return nt(got, fold_matrix(heads, dim, chosen, n * dim))

    def spread(x):
        return nn(pick, jnp.where(own, x, 0.0).astype(BF))

    def put(n, block, target, x):
        block[...] = x.astype(BF)
        copy = pltpu.make_async_copy(block, target, store_sem.at[n])
        copy.start()
        return copy

    dk_far, dv_far = spread(returned(1)), spread(returned(2))
    loads[3].wait()
    dq = spread(tn(ds, k_ref[...]) * scale + returned(0))
    loads[4].wait()
    stores = [put(0, dq_ref, dq_hbm, dql[...].astype(F32) + dq)]
    loads[5].wait()
    dk = nn(ds, qb[...]) * scale + dk_far
    loads[6].wait()
    stores.append(put(1, dk_ref, dk_hbm, dkl[...].astype(F32) + dk))
    loads[7].wait()
    dv = nn(w, gb[...]) + dv_far
    loads[8].wait()
    stores.append(put(2, dv_ref, dv_hbm, dvl[...].astype(F32) + dv))
    for copy in stores:
        copy.wait()


def shards(queries, keys, values, grad_out, local_span, head_residue, valid_count):
    tokens, width = queries.shape
    heads = local_span.shape[0]
    chosen = heads * (tokens // STEP)
    assert heads == WINDOW and chosen == tokens
    smem = pl.BlockSpec(memory_space=pltpu.SMEM)
    hbm = pl.BlockSpec(memory_space=pltpu.MemorySpace.HBM)
    full = ((tokens, width), BF)
    turned = ((width, tokens), BF)
    pair = ((tokens, chosen), F32)
    block = ((chosen, chosen), BF)
    out = jax.ShapeDtypeStruct(*full)
    between = (block, pair, pair, full, full, full, full, full)
    back, pb, dpb, qb, gb, dql, dkl, dvl = pl.pallas_call(
        kernel,
        out_shape=tuple(jax.ShapeDtypeStruct(*x) for x in between),
        in_specs=[smem] * 3 + [hbm] * 4,
        out_specs=(hbm,) * 8,
        scratch_shapes=[pltpu.VMEM(*full)] * 4
        + [
            pltpu.SemaphoreType.DMA((4,)),
            pltpu.SemaphoreType.DMA((7,)),
            pltpu.SemaphoreType.DMA((1,)),
        ]
        + [pltpu.VMEM(*turned)] * 4
        + [pltpu.VMEM((width, tokens), F32)] * 3
        + [pltpu.VMEM(*full)] * 5
        + [pltpu.VMEM((tokens, tokens), jnp.int32)]
        + [pltpu.VMEM(*pair)] * 2
        + [pltpu.VMEM(*block)] * 3
        + [pltpu.SemaphoreType.DMA((WINDOW,))] * 4,
        compiler_params=pltpu.CompilerParams(
            collective_id=0, has_side_effects=True, vmem_limit_bytes=VMEM_LIMIT
        ),
    )(local_span, head_residue, valid_count, queries, keys, values, grad_out)
    return pl.pallas_call(
        finish,
        out_shape=(out, out, out),
        in_specs=[smem] + [hbm] * 9,
        out_specs=(hbm, hbm, hbm),
        scratch_shapes=[pltpu.VMEM(*block), pltpu.VMEM(*pair), pltpu.VMEM(*pair)]
        + [pltpu.VMEM(*full)] * 9
        + [pltpu.SemaphoreType.DMA((9,)), pltpu.SemaphoreType.DMA((3,))],
        compiler_params=pltpu.CompilerParams(vmem_limit_bytes=VMEM_LIMIT),
    )(head_residue, back, pb, dpb, keys, dql, qb, dkl, gb, dvl)


def solution(mesh):
    rows = P(("groups", "seq"), None)
    return jax.shard_map(
        shards,
        mesh=mesh,
        in_specs=(rows, rows, rows, rows, P(), P(), P("groups")),
        out_specs=(rows, rows, rows),
        check_vma=False,
    )
```

```python
import math

import jax
import jax.numpy as jnp
from jax import lax
from jax.experimental import pallas as pl
from jax.experimental.pallas import tpu as pltpu
from jax.sharding import PartitionSpec as P

STEP = 16
WINDOW = 16
FLOOR = -1e30
LOG2E = 1.4426950408889634
EARLY_HEADS = 8
VMEM_LIMIT = 63 * 2**20

BF = jnp.bfloat16
F32 = jnp.float32


def nn(a, b):
    return lax.dot_general(a, b, (((1,), (0,)), ((), ())), preferred_element_type=F32)


def nt(a, b):
    return lax.dot_general(a, b, (((1,), (1,)), ((), ())), preferred_element_type=F32)


def tn(a, b):
    return lax.dot_general(a, b, (((0,), (0,)), ((), ())), preferred_element_type=F32)


def parts_of(x, count):
    out = []
    for _ in range(count - 1):
        head = x.astype(BF).astype(F32)
        out.append(head)
        x = x - head
    out.append(x)
    return out


def rows_block(rows, height, width):
    at = lax.broadcasted_iota(jnp.int32, (height, width), 0)
    block = jnp.zeros((height, width), F32)
    for n, row in enumerate(rows):
        block = jnp.where(at == n, row, block)
    return block


def kernel(
    span_ref, res_ref, count_ref, q_hbm, k_hbm, v_hbm, g_hbm,
    dq_hbm, dk_hbm, dv_hbm,
    dq_ref, dk_ref, dv_ref, store_sem, q_ref, k_ref, v_ref, g_ref, load_sem, qt, kt, vt, gt, dqt, dkt, dvt, qb, gb, pick, far, pb, dpb,
    send1, recv1, send2, recv2, ss1, rs1, ss2, rs2,
):
    tokens, width = q_ref.shape
    heads = span_ref.shape[0]
    dim = width // heads
    few = tokens // STEP
    chosen = heads * few
    scale = 1.0 / math.sqrt(dim)
    scale2 = scale * LOG2E
    me = lax.axis_index("seq")
    base = (me // WINDOW) * WINDOW
    my = me - base
    count = count_ref[0]
    loads = [
        pltpu.make_async_copy(source, target, load_sem.at[n])
        for n, (source, target) in enumerate(
            ((q_hbm, q_ref), (g_hbm, g_ref), (k_hbm, k_ref), (v_hbm, v_ref))
        )
    ]
    for load in loads:
        load.start()

    def partner(n):
        return lax.rem(my + n, WINDOW)

    barrier = pltpu.get_barrier_semaphore()

    def greet(n, carry):
        pl.semaphore_signal(
            barrier, inc=1, device_id={"seq": base + partner(n)},
            device_id_type=pl.DeviceIdType.MESH,
        )
        return carry

    lax.fori_loop(1, WINDOW, greet, 0)

    def block_of(n):
        return pl.ds(pl.multiple_of(n * few, few), few)

    def exchange(n, source, target, send_sem, recv_sem):
        to = partner(n)
        return pltpu.make_async_remote_copy(
            src_ref=source.at[block_of(to)],
            dst_ref=target.at[block_of(my)],
            send_sem=send_sem.at[n],
            recv_sem=recv_sem.at[n],
            device_id={"seq": base + to},
            device_id_type=pl.DeviceIdType.MESH,
        )

    def start_all(*args):
        def step(n, carry):
            exchange(n, *args).start()
            return carry

        lax.fori_loop(1, WINDOW, step, 0)

    def wait_all(*args):
        def step(n, carry):
            exchange(n, *args).wait_recv()
            return carry

        lax.fori_loop(1, WINDOW, step, 0)

    def wait_sent(*args):
        def step(n, carry):
            exchange(n, *args).wait_send()
            return carry

        lax.fori_loop(1, WINDOW, step, 0)

    lane = lax.broadcasted_iota(jnp.int32, (1, chosen), 1)
    lane_head = lane // few
    lane_res = jnp.zeros((1, chosen), jnp.int32)
    lane_span = jnp.zeros((1, chosen), jnp.int32)
    for h in range(heads):
        lane_res = jnp.where(lane_head == h, res_ref[h], lane_res)
        lane_span = jnp.where(lane_head == h, span_ref[h], lane_span)
    lane_token = (lane % few) * STEP + lane_res
    row = lax.broadcasted_iota(jnp.int32, (tokens, tokens), 0)
    col = lax.broadcasted_iota(jnp.int32, (tokens, tokens), 1)
    start = me * tokens
    huge = jnp.int32(1 << 20)
    row_ok = row + start < count
    far[...] = jnp.where(row_ok, row ^ col, huge)
    pick[...] = (row == lane_token).astype(F32).astype(BF)

    for load, source, target in zip(
        loads, (q_ref, g_ref, k_ref, v_ref), (qt, gt, kt, vt)
    ):
        load.wait()
        target[...] = source[...].T

    def picked(source, keep):
        full = nn(source[...], pick[...])
        total = jnp.zeros((dim, chosen), F32)
        for h in range(heads):
            part = jnp.where(lane_head == h, full[h * dim : (h + 1) * dim], 0.0)
            if keep is not None:
                keep[h * dim : (h + 1) * dim, :] = part.astype(BF)
            total = total + part
        return total

    q_few = picked(qt, qb)
    g_few = picked(gt, gb)
    k_few = picked(kt, None)
    v_few = picked(vt, None)

    mask = jnp.where(row_ok, row ^ lane_token, huge) < lane_span
    s = jnp.where(mask, nn(k_ref[...], qb[...]) * scale2, FLOOR)
    top = jnp.max(s, axis=0, keepdims=True)
    p = jnp.exp2(s - top)
    total = jnp.sum(p, axis=0, keepdims=True)
    p = p * (1.0 / total)
    dp = nn(v_ref[...], gb[...])
    local_lse = top + jnp.log(total) * LOG2E
    local_delta = jnp.sum(p * dp, axis=0, keepdims=True)
    pb[...] = p
    dpb[...] = dp
    tail = chosen - 4 * dim
    stats = rows_block(parts_of(local_lse, 3) + parts_of(local_delta, 2), tail, chosen)
    packed = jnp.concatenate([q_few, k_few, v_few, g_few, stats], axis=0)
    send1[...] = packed.T.astype(BF)

    pl.semaphore_wait(barrier, WINDOW - 1)
    start_all(send1, recv1, ss1, rs1)
    recv1[block_of(my), :] = send1[block_of(my), :]

    query_ok = lane + start < count

    def local_head(h, carry):
        at = pl.ds(pl.multiple_of(h * dim, 16), dim)
        qh, kh, vh, gh = qt[at, :], kt[at, :], vt[at, :], gt[at, :]
        s = jnp.where(far[...] < span_ref[h], tn(kh, qh) * scale2, FLOOR)
        top = jnp.max(s, axis=0, keepdims=True)
        p = jnp.exp2(s - top)
        inverse = 1.0 / jnp.sum(p, axis=0, keepdims=True)
        dp = tn(vh, gh)
        delta = jnp.sum(p * dp, axis=0, keepdims=True) * inverse
        keep = query_ok & (lane % STEP != res_ref[h])
        w = p * jnp.where(keep, inverse, 0.0)
        ds = (w * (dp - delta)).astype(BF)
        dqt[at, :] = nn(kh, ds) * scale
        dkt[at, :] = nt(qh, ds) * scale
        dvt[at, :] = nt(gh, w.astype(BF))
        return carry

    lax.fori_loop(0, EARLY_HEADS, local_head, 0, unroll=4)

    wait_all(send1, recv1, ss1, rs1)
    got = recv1[...].astype(F32).T
    got_half = got.astype(BF)
    qh, kh = got_half[0:dim], got_half[dim : 2 * dim]
    vh, gh = got_half[2 * dim : 3 * dim], got_half[3 * dim : 4 * dim]
    at = 4 * dim
    local_lse = got[at : at + 1] + got[at + 1 : at + 2] + got[at + 2 : at + 3]
    local_delta = got[at + 3 : at + 4] + got[at + 4 : at + 5]
    limit = count - base * tokens - res_ref[my]
    s = jnp.where(row * STEP < limit, tn(kh, qh) * scale2, FLOOR)
    top = jnp.max(s, axis=0, keepdims=True)
    p = jnp.exp2(s - top)
    total = jnp.sum(p, axis=0, keepdims=True)
    dilated_lse = top + jnp.log(total) * LOG2E
    most = jnp.maximum(local_lse, dilated_lse)
    both = most + jnp.log(jnp.exp2(local_lse - most) + jnp.exp2(dilated_lse - most)) * LOG2E
    here_ok = lane * STEP < limit
    local_part = jnp.where(here_ok, jnp.exp2(local_lse - both), 0.0)
    u = p * jnp.where(here_ok, jnp.exp2(top - both), 0.0)
    dp = tn(vh, gh)
    delta = local_part * local_delta + jnp.sum(u * dp, axis=0, keepdims=True)
    delta = jnp.where(here_ok, delta, 0.0)
    ds = (u * (dp - delta)).astype(BF)
    stats = rows_block(parts_of(local_part, 2) + parts_of(delta, 2), chosen - 3 * dim, chosen)
    packed = jnp.concatenate(
        [nn(kh, ds) * scale, nt(qh, ds) * scale, nt(gh, u.astype(BF)), stats], axis=0
    )
    send2[...] = packed.T.astype(BF)
    start_all(send2, recv2, ss2, rs2)
    recv2[block_of(my), :] = send2[block_of(my), :]

    lax.fori_loop(EARLY_HEADS, heads, local_head, 0, unroll=4)

    wait_all(send2, recv2, ss2, rs2)
    back = recv2[...].astype(F32).T
    at = 3 * dim
    local_part = back[at : at + 1] + back[at + 1 : at + 2]
    delta = back[at + 2 : at + 3] + back[at + 3 : at + 4]
    w = pb[...] * local_part
    ds = (w * (dpb[...] - delta)).astype(BF)
    wide = nn(kt[...], ds) * scale
    dq_few, dk_few, dv_few = back[0:dim], back[dim : 2 * dim], back[2 * dim : 3 * dim]

    def spread(piece_of):
        pieces = [
            jnp.where(lane_head == h, piece_of(h), 0.0).astype(BF) for h in range(heads)
        ]
        return nt(jnp.concatenate(pieces, axis=0), pick[...])

    def store(n, source, target):
        copy = pltpu.make_async_copy(source, target, store_sem.at[n])
        copy.start()
        return copy

    dq = dqt[...] + spread(lambda h: wide[h * dim : (h + 1) * dim] + dq_few)
    dq_ref[...] = dq.astype(BF)
    store_dq = store(0, dq_ref, dq_hbm)
    dk = dkt[...] + nt(qb[...], ds) * scale + spread(lambda h: dk_few)
    dk_ref[...] = dk.astype(BF)
    store_dk = store(1, dk_ref, dk_hbm)
    dv = dvt[...] + nt(gb[...], w.astype(BF)) + spread(lambda h: dv_few)
    dv_ref[...] = dv.astype(BF)
    store_dv = store(2, dv_ref, dv_hbm)
    wait_sent(send1, recv1, ss1, rs1)
    wait_sent(send2, recv2, ss2, rs2)
    store_dq.wait()
    store_dk.wait()
    store_dv.wait()


def finish(a_in, b_in, c_in, a_out, b_out, c_out, sources, targets, load_sem, store_sem):
    loads = [
        pltpu.make_async_copy(ref, sources.at[n], load_sem.at[n])
        for n, ref in enumerate((a_in, b_in, c_in))
    ]
    for load in loads:
        load.start()
    stores = [
        pltpu.make_async_copy(targets.at[n], ref, store_sem.at[n])
        for n, ref in enumerate((a_out, b_out, c_out))
    ]
    for n in range(3):
        loads[n].wait()
        targets[n] = sources[n].T
        stores[n].start()
    for store in stores:
        store.wait()


def shards(queries, keys, values, grad_out, local_span, head_residue, valid_count):
    tokens, width = queries.shape
    heads = local_span.shape[0]
    chosen = heads * (tokens // STEP)
    assert heads == WINDOW and chosen == tokens
    smem = pl.BlockSpec(memory_space=pltpu.SMEM)
    vmem = pl.BlockSpec(memory_space=pltpu.VMEM)
    hbm = pl.BlockSpec(memory_space=pltpu.MemorySpace.HBM)
    out = jax.ShapeDtypeStruct((tokens, width), BF)
    turned = jax.ShapeDtypeStruct((width, tokens), BF)
    gradients = pl.pallas_call(
        kernel,
        out_shape=(turned, turned, turned),
        in_specs=[smem] * 3 + [hbm] * 4,
        out_specs=(hbm, hbm, hbm),
        scratch_shapes=[pltpu.VMEM((width, tokens), BF)] * 3
        + [pltpu.SemaphoreType.DMA((3,))]
        + [pltpu.VMEM((tokens, width), BF)] * 4
        + [pltpu.SemaphoreType.DMA((4,))]
        + [pltpu.VMEM((width, tokens), BF)] * 4
        + [pltpu.VMEM((width, tokens), F32)] * 3
        + [pltpu.VMEM((width, chosen), BF)] * 2
        + [
            pltpu.VMEM((tokens, chosen), BF),
            pltpu.VMEM((tokens, tokens), jnp.int32),
            pltpu.VMEM((tokens, chosen), F32),
            pltpu.VMEM((tokens, chosen), F32),
        ]
        + [pltpu.VMEM((chosen, chosen), BF)] * 4
        + [pltpu.SemaphoreType.DMA((WINDOW,))] * 4,
        compiler_params=pltpu.CompilerParams(
            collective_id=0, has_side_effects=True, vmem_limit_bytes=VMEM_LIMIT
        ),
    )(local_span, head_residue, valid_count, queries, keys, values, grad_out)
    return pl.pallas_call(
        finish,
        out_shape=(out, out, out),
        in_specs=[hbm] * 3,
        out_specs=(hbm, hbm, hbm),
        scratch_shapes=[
            pltpu.VMEM((3, width, tokens), BF),
            pltpu.VMEM((3, tokens, width), BF),
            pltpu.SemaphoreType.DMA((3,)),
            pltpu.SemaphoreType.DMA((3,)),
        ],
        compiler_params=pltpu.CompilerParams(vmem_limit_bytes=VMEM_LIMIT),
    )(*gradients)


def solution(mesh):
    rows = P(("groups", "seq"), None)
    return jax.shard_map(
        shards,
        mesh=mesh,
        in_specs=(rows, rows, rows, rows, P(), P(), P("groups")),
        out_specs=(rows, rows, rows),
        check_vma=False,
    )
```
